32 devices in a mesh: pb: 8 (over z, y), ka: 4 (over x, core).
Axes of the slice: x: 2, y: 2, z: 4, core: 2. Of those that a mesh axis runs over, the one named last changes fastest.
Arguments:
- pair_trunk: bfloat16 [384, 384, 128], P('pb', 'ka'), may hold values from -40 to 40
- token_ids: int32 [3, 384], replicated, may hold values from 0 to 422, as said below
- w_rel: bfloat16 [139, 128], replicated, may hold values from -3.5 to 3.5
- cat_gain: float32 [256], replicated, may hold values from 0.1 to 1.9
- w_in: bfloat16 [256, 128], replicated, may hold values from -0.375 to 0.375
- trans_gain: float32 [2, 128], replicated, may hold values from 0.1 to 1.9
- trans_ab: bfloat16 [2, 128, 512], replicated, may hold values from -0.5 to 0.5
- trans_out: bfloat16 [2, 256, 128], replicated, may hold values from -0.375 to 0.375
- bias_gain: float32 [128], replicated, may hold values from 0.1 to 1.9
- w_bias: bfloat16 [128, 16], replicated, may hold values from -1.5 to 1.5
- normed: bfloat16 [8, 384, 768], P(None, 'pb', 'ka'), may hold values from -12 to 12
- w_proj: bfloat16 [4, 768, 768], P(None, None, 'ka'), may hold values from -1 to 1
- output_weight: bfloat16 [768, 768], P('ka'), may hold values from -0.21875 to 0.21875
Outputs:
- pair_cond: bfloat16 [384, 384, 128], P('pb', 'ka')
- update: bfloat16 [8, 384, 768], P(None, 'pb', 'ka')
The draws below stay inside these ranges and needn't reach their ends.
Inputs may be any that keep to these rules, and one draw needn't show every extreme that they name: `token_ids`: row 0 is a token's residue number, row 1 its chain number, row 2 its entity number. Chain numbers start at 0 and never fall along the tokens; residue numbers never fall within a chain; all tokens of a chain share one entity. The last token's residue number is 422.
All inputs are finite; a program needn't handle non-finite values.
Results may differ from the reference program's by a relative error of at most 0.015.
The reference program's roundings to bfloat16 on the way count: a program that leaves them out, or rounds other values in their place, can miss the bound.
Values may be sent and summed in bfloat16 or wider, within the bound.
A program may use at most 64 MiB of HBM per device.

```python
import jax
import jax.numpy as jnp
from jax import lax

D = 768
HEADS = 16
HD = 48
CZ = 128
HID = 256
RMAX = 32
SMAX = 2
REL = 139
S = 8
N = 384


def draw_pair_trunk(key, part):
    base_key = jax.random.fold_in(key, 0)
    values = jax.random.normal(base_key, (N, N, CZ), jnp.float32)
    return jnp.clip(values, -40.0, 40.0).astype(jnp.bfloat16)


def draw_token_ids(key, part):
    start_key, res_key, off_key, ent_key = jax.random.split(key, 4)
    places = jnp.arange(N, dtype=jnp.int32)
    period = max(N // 24, 2)
    starts = (jax.random.randint(start_key, (N,), 0, period) == 0) | (places == 0)
    chain_ids = jnp.cumsum(starts.astype(jnp.int32)) - 1
    first_place = lax.cummax(jnp.where(starts, places, 0), axis=0)
    fresh_res = (jax.random.randint(res_key, (N,), 0, 4) != 0) | starts
    counted = jnp.cumsum(fresh_res.astype(jnp.int32))
    offset = jax.random.randint(off_key, (N,), 0, 40)
    residue = counted - counted[first_place] + offset[chain_ids]
    residue = jnp.where(places == N - 1, N + 38, residue)
    entity = jax.random.randint(ent_key, (N,), 0, 4)[chain_ids]
    return jnp.stack([residue, chain_ids, entity]).astype(jnp.int32)


def draw_normed(key, part):
    base_key = jax.random.fold_in(key, 0)
    values = jax.random.normal(base_key, (S, N, D), jnp.float32)
    return jnp.clip(values, -12.0, 12.0).astype(jnp.bfloat16)


def draw_w_proj(key, part):
    base_key = jax.random.fold_in(key, 0)
    spread_scale = D ** (-0.5)
    weights = jax.random.normal(base_key, (4, D, D), jnp.float32) * spread_scale
    return jnp.clip(weights, -1.0, 1.0).astype(jnp.bfloat16)


def steps_of(rng, extent, shards, least, top_value):
    level = 1.0
    for position, blocks in shards:
        heights = jax.random.uniform(jax.random.fold_in(jax.random.fold_in(rng, 6), position), (blocks,), jnp.float32, least / len(shards), top_value / len(shards))
        level = level * jnp.repeat(jnp.exp(heights), extent[position] // blocks).reshape((-1,) + (1,) * (len(extent) - 1 - position))
    return level


def normal_values(own_key, shape, width, limit, shards=(), kind=jnp.bfloat16):
    result = jax.random.normal(own_key, shape, jnp.float32) * width
    if len(shards) > 0:
        result = steps_of(own_key, shape, shards, -0.22, 0.18) * result
    return jnp.clip(result, min=-limit, max=limit).astype(kind)


def setup_inputs(seed: int = 0) -> dict:
    splits = jax.random.split(jax.random.key(seed), 14)
    return {
        "pair_trunk": draw_pair_trunk(jax.random.fold_in(splits[13], 71), 0),
        "token_ids": draw_token_ids(jax.random.fold_in(splits[13], 71), 0),
        "w_rel": normal_values(splits[2], (REL, CZ), 3 ** -0.5, 3.5),
        "cat_gain": jnp.clip(1.0 + 0.18 * jax.random.normal(splits[3], (2 * CZ,), jnp.float32), 0.1, 1.9),
        "w_in": normal_values(splits[4], (2 * CZ, CZ), (2 * CZ) ** -0.5, 0.375),
        "trans_gain": jnp.clip(1.0 + 0.18 * jax.random.normal(splits[5], (2, CZ), jnp.float32), 0.1, 1.9),
        "trans_ab": normal_values(splits[6], (2, CZ, 2 * HID), CZ ** -0.5, 0.5),
        "trans_out": normal_values(splits[7], (2, HID, CZ), HID ** -0.5, 0.375),
        "bias_gain": jnp.clip(1.0 + 0.18 * jax.random.normal(splits[8], (CZ,), jnp.float32), 0.1, 1.9),
        "w_bias": normal_values(splits[9], (CZ, HEADS), (CZ // 8) ** -0.5, 1.5),
        "normed": draw_normed(jax.random.fold_in(splits[13], 71), 0),
        "w_proj": draw_w_proj(jax.random.fold_in(splits[13], 71), 0),
        "output_weight": normal_values(splits[12], (D, D), D ** -0.5, 0.21875, ((0, 4),)),
    }


EPS = 1e-05

def layer_norm(values, scaling):
    average = lax.optimization_barrier(jnp.mean(values, axis=-1, keepdims=True))
    centered = values - average
    spread = lax.optimization_barrier(jnp.mean(centered * centered, axis=-1, keepdims=True))
    return centered * lax.rsqrt(spread + EPS) * scaling

def relative_onehot(query_token_ids, key_ids, query_pos, key_pos):
    query_res = query_token_ids[0][:, None]
    key_res = key_ids[0][None, :]
    query_chain = query_token_ids[1][:, None]
    key_chain = key_ids[1][None, :]
    query_entity = query_token_ids[2][:, None]
    key_ent = key_ids[2][None, :]
    same_chain = query_chain == key_chain
    same_res = same_chain & (query_res == key_res)
    same_entity = query_entity == key_ent
    res_bins = 2 * RMAX + 2
    res_bin = jnp.where(same_chain, jnp.clip(query_res - key_res + RMAX, 0, 2 * RMAX), 2 * RMAX + 1)
    token_offset_bin = jnp.where(same_res, jnp.clip(query_pos[:, None] - key_pos[None, :] + RMAX, 0, 2 * RMAX), 2 * RMAX + 1)
    chain_offset_bin = jnp.where(same_entity, jnp.clip(query_chain - key_chain + SMAX, 0, 2 * SMAX), 2 * SMAX + 1)
    columns = jnp.arange(REL, dtype=jnp.int32)
    onehot = (columns == res_bin[..., None]) | (columns == (res_bins + token_offset_bin)[..., None])
    onehot = onehot | (columns == (2 * res_bins + chain_offset_bin)[..., None])
    onehot = onehot | (columns == REL - 1) & same_entity[..., None]
    return onehot.astype(jnp.bfloat16)

def condition_block(trunk_blk, onehot, w_rel, cat_gain, w_in, trans_gain, trans_ab, trans_out, bias_gain, w_bias):
    half = trans_out.shape[1]
    relative = jnp.einsum('rkf,fc->rkc', onehot.astype(jnp.float32), w_rel.astype(jnp.float32))
    joined = jnp.concatenate([trunk_blk.astype(jnp.float32), relative], axis=-1)
    normal_in = layer_norm(joined, cat_gain).astype(jnp.bfloat16)
    pair_state = jnp.einsum('rkf,fc->rkc', normal_in.astype(jnp.float32), w_in.astype(jnp.float32))
    for layer_idx in range(2):
        normal_tr = layer_norm(pair_state, trans_gain[layer_idx]).astype(jnp.bfloat16)
        gate_up = jnp.einsum('rkc,cf->rkf', normal_tr.astype(jnp.float32), trans_ab[layer_idx].astype(jnp.float32))
        hidden = (jax.nn.silu(gate_up[..., :half]) * gate_up[..., half:]).astype(jnp.bfloat16)
        pair_state = pair_state + jnp.einsum('rkf,fc->rkc', hidden.astype(jnp.float32), trans_out[layer_idx].astype(jnp.float32))
    normal_b = layer_norm(pair_state, bias_gain).astype(jnp.bfloat16)
    bias_blk = jnp.einsum('rkc,ch->hrk', normal_b.astype(jnp.float32), w_bias.astype(jnp.float32)).astype(jnp.bfloat16)
    return (pair_state.astype(jnp.bfloat16), bias_blk)

def soft_weights(logits):
    row_max = lax.optimization_barrier(jnp.max(logits, axis=-1, keepdims=True))
    expweights = jnp.exp(logits - row_max)
    return (expweights / lax.optimization_barrier(jnp.sum(expweights, axis=-1, keepdims=True))).astype(jnp.bfloat16)

def reference(pair_trunk, token_ids, w_rel, cat_gain, w_in, trans_gain, trans_ab, trans_out, bias_gain, w_bias, normed, w_proj, output_weight):
    block_rows = 16
    positions = jnp.arange(N, dtype=jnp.int32)

    def one_block(block_idx):
        begin_at = (block_idx * block_rows).astype(jnp.int32)
        trunk_blk = lax.dynamic_slice_in_dim(pair_trunk, begin_at, block_rows, 0)
        query_token_ids = lax.dynamic_slice_in_dim(token_ids, begin_at, block_rows, 1)
        query_pos = begin_at + jnp.arange(block_rows, dtype=jnp.int32)
        onehot = relative_onehot(query_token_ids, token_ids, query_pos, positions)
        return condition_block(trunk_blk, onehot, w_rel, cat_gain, w_in, trans_gain, trans_ab, trans_out, bias_gain, w_bias)
    pair_blocks, bias_blocks = lax.map(one_block, jnp.arange(N // block_rows, dtype=jnp.int32))
    pair_out = pair_blocks.reshape(N, N, CZ)
    bias_all = jnp.transpose(bias_blocks, (1, 0, 2, 3)).reshape(HEADS, N, N)
    projected = jnp.einsum('snd,pde->psne', normed.astype(jnp.float32), w_proj.astype(jnp.float32))
    query_all = jnp.transpose(projected[0].astype(jnp.bfloat16).reshape(S, N, HEADS, HD), (2, 0, 1, 3))
    key_all = jnp.transpose(projected[1].astype(jnp.bfloat16).reshape(S, N, HEADS, HD), (2, 0, 1, 3))
    value_all = jnp.transpose(projected[2].astype(jnp.bfloat16).reshape(S, N, HEADS, HD), (2, 0, 1, 3))
    scale_factor = HD ** (-0.5)

    def one_head(inputs):
        query_per_head, key_h, value_h, bias_h = inputs
        logits = jnp.einsum('sqd,skd->sqk', query_per_head.astype(jnp.float32), key_h.astype(jnp.float32)) * scale_factor
        logits = logits + bias_h.astype(jnp.float32)[None]
        weights = soft_weights(logits)
        return jnp.einsum('sqk,skd->sqd', weights.astype(jnp.float32), value_h.astype(jnp.float32))
    heads_out = lax.map(one_head, (query_all, key_all, value_all, bias_all))
    attended = jnp.transpose(heads_out, (1, 2, 0, 3)).reshape(S, N, D)
    gated_result = (attended * jax.nn.sigmoid(projected[3])).astype(jnp.bfloat16)
    update = jnp.einsum('fja,ac->fjc', gated_result.astype(jnp.float32), output_weight.astype(jnp.float32)).astype(jnp.bfloat16)
    return (pair_out, update)
```

```python
import math
import functools

import jax
import jax.numpy as jnp
from jax import lax
from jax.experimental import pallas as pl
from jax.experimental.pallas import tpu as pltpu
from jax.sharding import PartitionSpec as P

HD = 48
RMAX = 32
SMAX = 2
REL = 139
EPS = 1e-05
F32 = jnp.float32
BF16 = jnp.bfloat16
ROWS = 16


def dot(a, b):
    return jnp.dot(a, b, preferred_element_type=F32)


def norm_rows(v, gain):
    centered = v - jnp.mean(v, axis=-1, keepdims=True)
    spread = jnp.mean(centered * centered, axis=-1, keepdims=True)
    return (centered * lax.rsqrt(spread + EPS) * gain).astype(BF16)


def onehot_row(q_res, q_chain, q_ent, q_pos, k_res, k_chain, k_ent, k_pos):
    shape = k_res.shape
    lane = lax.broadcasted_iota(jnp.int32, shape, 1)
    bins = 2 * RMAX + 2
    same_chain = k_chain == q_chain
    same_res = same_chain & (k_res == q_res)
    same_ent = k_ent == q_ent
    res_bin = jnp.where(same_chain, jnp.clip((q_res + RMAX) - k_res, 0, 2 * RMAX), bins - 1)
    tok_bin = jnp.where(
        same_res,
        jnp.clip((q_pos + (RMAX + bins)) - k_pos, bins, bins + 2 * RMAX),
        2 * bins - 1,
    )
    chain_bin = jnp.where(
        same_ent,
        jnp.clip((q_chain + (SMAX + 2 * bins)) - k_chain, 2 * bins, 2 * bins + 2 * SMAX),
        2 * bins + 2 * SMAX + 1,
    )
    low = (lane == res_bin) | (lane == tok_bin)
    high_lane = lane + 128
    high = (high_lane == tok_bin) | (high_lane == chain_bin)
    high = high | ((high_lane == REL - 1) & same_ent)
    one = jnp.where(low, 1.0, 0.0)
    two = jnp.where(high, 1.0, 0.0)
    return jnp.concatenate([one, two], axis=-1).astype(BF16)


def pair_block(
    begin,
    q_start,
    k_pos,
    tok_ref,
    key_ref,
    trunk_ref,
    wrel_scr,
    cat_gain_ref,
    w_in_ref,
    trans_gain_ref,
    ab_ref,
    out_ref,
    bias_gain_ref,
    w_bias_ref,
    pair_ref,
    bias_scr,
    bias_ref,
):
    keys = trunk_ref.shape[1]
    c = trunk_ref.shape[2]
    k_res, k_chain, k_ent = key_ref[0], key_ref[1], key_ref[2]
    rows = []
    for r in range(ROWS):
        at = q_start + begin + r
        rows.append(
            onehot_row(
                tok_ref[0, at], tok_ref[1, at], tok_ref[2, at], at, k_res, k_chain, k_ent, k_pos
            )
        )
    onehot = jnp.concatenate(rows, axis=0)
    rel = dot(onehot, wrel_scr[...])
    trunk = trunk_ref[pl.ds(begin, ROWS)].reshape(ROWS * keys, c).astype(F32)
    mean = jnp.sum(trunk + rel, axis=-1, keepdims=True) * (1.0 / (2 * c))
    ct = trunk - mean
    cr = rel - mean
    var = jnp.sum(ct * ct + cr * cr, axis=-1, keepdims=True) * (1.0 / (2 * c))
    inv = lax.rsqrt(var + EPS)
    gain = cat_gain_ref[...]
    normal_in = jnp.concatenate(
        [(ct * inv * gain[:, :c]).astype(BF16), (cr * inv * gain[:, c:]).astype(BF16)], axis=-1
    )
    state = dot(normal_in, w_in_ref[...])
    half = out_ref.shape[1]
    for l in range(2):
        normal = norm_rows(state, trans_gain_ref[l : l + 1, :])
        gate_up = dot(normal, ab_ref[l])
        gate_half = gate_up[:, :half] * 0.5
        silu = gate_half + gate_half * jnp.tanh(gate_half)
        hidden = (silu * gate_up[:, half:]).astype(BF16)
        state = state + dot(hidden, out_ref[l])
    pair_ref[pl.ds(begin, ROWS)] = state.astype(BF16).reshape(ROWS, keys, c)
    normal_b = norm_rows(state, bias_gain_ref[...])
    for r in range(ROWS):
        bias_scr[:, r, :] = lax.dot_general(
            w_bias_ref[...],
            normal_b[r * keys : (r + 1) * keys],
            (((0,), (1,)), ((), ())),
            preferred_element_type=F32,
        )
    bias_ref[:, pl.ds(begin, ROWS), :] = bias_scr[...].astype(BF16)


def pair_kernel(
    tok_ref, key_ref, trunk_ref, w_rel_ref, cat_gain_ref, w_in_ref, trans_gain_ref, ab_ref,
    out_ref, bias_gain_ref, w_bias_ref, pair_ref, bias_ref, wrel_scr, bias_scr,
):
    q_rows, keys = trunk_ref.shape[0], trunk_ref.shape[1]
    q_start = lax.axis_index("pb") * q_rows
    k_start = lax.axis_index("ka") * keys
    wrel_scr[...] = jnp.zeros_like(wrel_scr)
    wrel_scr[0:REL, :] = w_rel_ref[...]
    k_pos = k_start + lax.broadcasted_iota(jnp.int32, key_ref.shape[1:], 0)

    def step(i, carry):
        pair_block(
            pl.multiple_of(i * ROWS, ROWS), q_start, k_pos, tok_ref, key_ref, trunk_ref, wrel_scr,
            cat_gain_ref, w_in_ref, trans_gain_ref, ab_ref, out_ref, bias_gain_ref, w_bias_ref,
            pair_ref, bias_scr, bias_ref,
        )
        return carry

    lax.fori_loop(0, q_rows // ROWS, step, 0)


def pair_call(token_ids, key_cols, trunk, w_rel, cat_gain, w_in, trans_gain, ab, out, bias_gain, w_bias):
    q_rows, keys, c = trunk.shape
    heads = w_bias.shape[1]
    vmem = pl.BlockSpec(memory_space=pltpu.VMEM)
    return pl.pallas_call(
        pair_kernel,
        out_shape=(
            jax.ShapeDtypeStruct((q_rows, keys, c), BF16),
            jax.ShapeDtypeStruct((heads, q_rows, keys), BF16),
        ),
        in_specs=[pl.BlockSpec(memory_space=pltpu.SMEM)] + [vmem] * 10,
        out_specs=(vmem, vmem),
        scratch_shapes=[pltpu.VMEM((256, c), BF16), pltpu.VMEM((heads, ROWS, keys), F32)],
        compiler_params=pltpu.CompilerParams(vmem_limit_bytes=40 << 20),
        cost_estimate=pl.CostEstimate(flops=2300000000, bytes_accessed=4000000, transcendentals=0),
    )(token_ids, key_cols, trunk, w_rel, cat_gain.reshape(1, -1), w_in, trans_gain, ab, out,
      bias_gain.reshape(1, -1), w_bias)


def soft_weights(logits):
    row_max = jnp.max(logits, axis=-1, keepdims=True)
    expweights = jnp.exp(logits - row_max)
    return (expweights / jnp.sum(expweights, axis=-1, keepdims=True)).astype(jnp.bfloat16)


def shards(
    pair_trunk,
    token_ids,
    w_rel,
    cat_gain,
    w_in,
    trans_gain,
    trans_ab,
    trans_out,
    bias_gain,
    w_bias,
    normed,
    w_proj,
    output_weight,
):
    q_rows = pair_trunk.shape[0]
    k_rows = pair_trunk.shape[1]
    k_start = lax.axis_index("ka") * k_rows
    key_ids = lax.dynamic_slice_in_dim(token_ids, k_start, k_rows, 1)
    key_cols = jnp.broadcast_to(key_ids[:, :, None], (3, k_rows, 128))
    pair_cond, bias_tile = pair_call(
        token_ids, key_cols, pair_trunk, w_rel, cat_gain, w_in, trans_gain, trans_ab, trans_out,
        bias_gain, w_bias,
    )
    samples = normed.shape[0]
    feat_local = normed.shape[2]
    heads_local = feat_local // HD
    scale_factor = 1.0 / math.sqrt(HD)
    projected = jnp.einsum(
        "sqf,pfe->psqe",
        lax.all_gather(normed, "ka", axis=2, tiled=True),
        w_proj,
        preferred_element_type=jnp.float32,
    )
    queries = projected[0].astype(jnp.bfloat16).reshape(samples, q_rows, heads_local, HD)
    kv_local = jnp.transpose(
        jnp.stack([projected[1], projected[2]], axis=1).astype(jnp.bfloat16), (0, 1, 3, 2)
    )
    bias_rows = lax.all_to_all(bias_tile, "ka", split_axis=0, concat_axis=2, tiled=True)
    kv_all = lax.all_gather(kv_local, "pb", axis=3, tiled=True)
    keys_all = kv_all[:, 0].reshape(samples, heads_local, HD, kv_all.shape[3])
    values_all = kv_all[:, 1].reshape(samples, heads_local, HD, kv_all.shape[3])
    logits = (
        jnp.einsum("sqhd,shdk->shqk", queries, keys_all, preferred_element_type=jnp.float32)
        * scale_factor
    )
    logits = logits + bias_rows[None].astype(jnp.float32)
    weights = soft_weights(logits)
    attended = jnp.einsum(
        "shqk,shdk->sqhd", weights, values_all, preferred_element_type=jnp.float32
    )
    gated_result = (
        attended.reshape(samples, q_rows, feat_local) * jax.nn.sigmoid(projected[3])
    ).astype(jnp.bfloat16)
    flat_gated = gated_result.reshape(samples * q_rows, feat_local)
    summed = lax.psum_scatter(
        jnp.einsum(
            "fe,nf->en", output_weight, flat_gated, preferred_element_type=jnp.float32
        ).astype(jnp.bfloat16),
        "ka",
        scatter_dimension=0,
        tiled=True,
    ).astype(jnp.float32)
    update = jnp.transpose(summed).reshape(samples, q_rows, feat_local).astype(jnp.bfloat16)
    return (pair_cond, update)


def solution(mesh):
    in_specs = (
        P("pb", "ka", None),
        P(),
        P(),
        P(),
        P(),
        P(),
        P(),
        P(),
        P(),
        P(),
        P(None, "pb", "ka"),
        P(None, None, "ka"),
        P("ka", None),
    )
    out_specs = (P("pb", "ka", None), P(None, "pb", "ka"))
    return jax.shard_map(shards, mesh=mesh, in_specs=in_specs, out_specs=out_specs, check_vma=False)
```

```python
import math
import functools

import jax
import jax.numpy as jnp
from jax import lax
from jax.experimental import pallas as pl
from jax.experimental.pallas import tpu as pltpu
from jax.sharding import PartitionSpec as P

HD = 48
RMAX = 32
SMAX = 2
REL = 139
EPS = 1e-05
F32 = jnp.float32
BF16 = jnp.bfloat16
ROWS = 16


def dot(a, b):
    return jnp.dot(a, b, preferred_element_type=F32)


def norm_rows(v, gain):
    centered = v - jnp.mean(v, axis=-1, keepdims=True)
    spread = jnp.mean(centered * centered, axis=-1, keepdims=True)
    return (centered * lax.rsqrt(spread + EPS) * gain).astype(BF16)


def onehot_row(q_res, q_chain, q_ent, q_pos, k_res, k_chain, k_ent, k_pos):
    shape = k_res.shape
    lane = lax.broadcasted_iota(jnp.int32, shape, 1)
    bins = 2 * RMAX + 2
    same_chain = k_chain == q_chain
    same_res = same_chain & (k_res == q_res)
    same_ent = k_ent == q_ent
    res_bin = jnp.where(same_chain, jnp.clip((q_res + RMAX) - k_res, 0, 2 * RMAX), bins - 1)
    tok_bin = jnp.where(
        same_res,
        jnp.clip((q_pos + (RMAX + bins)) - k_pos, bins, bins + 2 * RMAX),
        2 * bins - 1,
    )
    chain_bin = jnp.where(
        same_ent,
        jnp.clip((q_chain + (SMAX + 2 * bins)) - k_chain, 2 * bins, 2 * bins + 2 * SMAX),
        2 * bins + 2 * SMAX + 1,
    )
    low = (lane == res_bin) | (lane == tok_bin)
    high_lane = lane + 128
    high = (high_lane == tok_bin) | (high_lane == chain_bin)
    high = high | ((high_lane == REL - 1) & same_ent)
    one = jnp.where(low, 1.0, 0.0)
    two = jnp.where(high, 1.0, 0.0)
    return jnp.concatenate([one, two], axis=-1).astype(BF16)


def pair_block(
    begin,
    q_start,
    k_pos,
    tok_ref,
    key_ref,
    trunk_ref,
    wrel_scr,
    cat_gain_ref,
    w_in_ref,
    trans_gain_ref,
    ab_ref,
    out_ref,
    bias_gain_ref,
    w_bias_ref,
    pair_ref,
    bias_scr,
    bias_ref,
):
    keys = trunk_ref.shape[1]
    c = trunk_ref.shape[2]
    k_res, k_chain, k_ent = key_ref[0], key_ref[1], key_ref[2]
    rows = []
    for r in range(ROWS):
        at = q_start + begin + r
        rows.append(
            onehot_row(
                tok_ref[0, at], tok_ref[1, at], tok_ref[2, at], at, k_res, k_chain, k_ent, k_pos
            )
        )
    onehot = jnp.concatenate(rows, axis=0)
    rel = dot(onehot, wrel_scr[...])
    trunk = trunk_ref[pl.ds(begin, ROWS)].reshape(ROWS * keys, c).astype(F32)
    mean = jnp.sum(trunk + rel, axis=-1, keepdims=True) * (1.0 / (2 * c))
    ct = trunk - mean
    cr = rel - mean
    var = jnp.sum(ct * ct + cr * cr, axis=-1, keepdims=True) * (1.0 / (2 * c))
    inv = lax.rsqrt(var + EPS)
    gain = cat_gain_ref[...]
    normal_in = jnp.concatenate(
        [(ct * inv * gain[:, :c]).astype(BF16), (cr * inv * gain[:, c:]).astype(BF16)], axis=-1
    )
    state = dot(normal_in, w_in_ref[...])
    half = out_ref.shape[1]
    for l in range(2):
        normal = norm_rows(state, trans_gain_ref[l : l + 1, :])
        gate_up = dot(normal, ab_ref[l])
        gate_half = gate_up[:, :half] * 0.5
        silu = gate_half + gate_half * jnp.tanh(gate_half)
        hidden = (silu * gate_up[:, half:]).astype(BF16)
        state = state + dot(hidden, out_ref[l])
    pair_ref[pl.ds(begin, ROWS)] = state.astype(BF16).reshape(ROWS, keys, c)
    normal_b = norm_rows(state, bias_gain_ref[...])
    for r in range(ROWS):
        bias_scr[:, r, :] = lax.dot_general(
            w_bias_ref[...],
            normal_b[r * keys : (r + 1) * keys],
            (((0,), (1,)), ((), ())),
            preferred_element_type=F32,
        )
    bias_ref[:, pl.ds(begin, ROWS), :] = bias_scr[...].astype(BF16)


MESH = pl.DeviceIdType.MESH


def ka_peer(offset):
    size = lax.axis_size("ka")
    return lax.rem(lax.axis_index("ka") + offset, size)


def ring_index(pos):
    n = lax.axis_size("pb")
    pos = lax.rem(pos + 2 * n, n)
    if n % 2:
        return pos
    return jnp.where(pos < n // 2, 2 * pos, 2 * (n - 1 - pos) + 1)


def ring_position(index):
    n = lax.axis_size("pb")
    if n % 2:
        return index
    half = index // 2
    return jnp.where(lax.rem(index, 2) == 0, half, n - 1 - half)


def gather_kernel(x_ref, o_ref, local_sem, send_sem, recv_sem):
    me = lax.axis_index("ka")
    pb = lax.axis_index("pb")
    size = lax.axis_size("ka")
    barrier = pltpu.get_barrier_semaphore()
    for d in range(1, size):
        pl.semaphore_signal(barrier, inc=1, device_id=(pb, ka_peer(d)), device_id_type=MESH)
    own = pltpu.make_async_copy(x_ref, o_ref.at[me], local_sem)
    own.start()
    pl.semaphore_wait(barrier, size - 1)
    copies = []
    for d in range(1, size):
        copy = pltpu.make_async_remote_copy(
            src_ref=x_ref,
            dst_ref=o_ref.at[me],
            send_sem=send_sem.at[d - 1],
            recv_sem=recv_sem.at[d - 1],
            device_id=(pb, ka_peer(d)),
            device_id_type=MESH,
        )
        copy.start()
        copies.append(copy)
    own.wait()
    for copy in copies:
        copy.wait()


def gather_call(x):
    size = lax.axis_size("ka")
    vmem = pl.BlockSpec(memory_space=pltpu.VMEM)
    return pl.pallas_call(
        gather_kernel,
        out_shape=jax.ShapeDtypeStruct((size,) + x.shape, x.dtype),
        in_specs=[vmem],
        out_specs=vmem,
        scratch_shapes=[
            pltpu.SemaphoreType.DMA,
            pltpu.SemaphoreType.DMA((size - 1,)),
            pltpu.SemaphoreType.DMA((size - 1,)),
        ],
        compiler_params=pltpu.CompilerParams(
            collective_id=0, has_side_effects=True, vmem_limit_bytes=16 << 20
        ),
    )(x)


def pair_kernel(
    tok_ref, key_ref, trunk_ref, w_rel_ref, cat_gain_ref, w_in_ref, trans_gain_ref, ab_ref,
    out_ref, bias_gain_ref, w_bias_ref, kv_ref, pair_ref, bias_out_ref, kv_out_ref, wrel_scr,
    bias_scr, bias_ref, local_sem, ring_send, ring_recv, bias_send, bias_recv,
):
    q_rows, keys = trunk_ref.shape[0], trunk_ref.shape[1]
    n = lax.axis_size("pb")
    size = lax.axis_size("ka")
    pb = lax.axis_index("pb")
    ka = lax.axis_index("ka")
    pos = ring_position(pb)
    right, left = ring_index(pos + 1), ring_index(pos + n - 1)

    barrier = pltpu.get_barrier_semaphore()
    for side in (left, right):
        pl.semaphore_signal(barrier, inc=1, device_id=(side, ka), device_id_type=MESH)
    for d in range(1, size):
        pl.semaphore_signal(barrier, inc=1, device_id=(pb, ka_peer(d)), device_id_type=MESH)
    own = pltpu.make_async_copy(kv_ref, kv_out_ref.at[pb], local_sem.at[0])
    own.start()
    own.wait()

    q_start = pb * q_rows
    k_start = ka * keys
    wrel_scr[...] = jnp.zeros_like(wrel_scr)
    wrel_scr[0:REL, :] = w_rel_ref[...]
    k_pos = k_start + lax.broadcasted_iota(jnp.int32, key_ref.shape[1:], 0)
    pl.semaphore_wait(barrier, 2 + size - 1)

    def to_right(s):
        slot = kv_out_ref.at[ring_index(pos + n - s)]
        return pltpu.make_async_remote_copy(
            src_ref=slot, dst_ref=slot, send_sem=ring_send.at[0, s], recv_sem=ring_recv.at[0, s],
            device_id=(right, ka), device_id_type=MESH,
        )

    def to_left(s):
        slot = kv_out_ref.at[ring_index(pos + s)]
        return pltpu.make_async_remote_copy(
            src_ref=slot, dst_ref=slot, send_sem=ring_send.at[1, s], recv_sem=ring_recv.at[1, s],
            device_id=(left, ka), device_id_type=MESH,
        )

    def pair_step(i):
        pair_block(
            pl.multiple_of(i * ROWS, ROWS), q_start, k_pos, tok_ref, key_ref, trunk_ref, wrel_scr,
            cat_gain_ref, w_in_ref, trans_gain_ref, ab_ref, out_ref, bias_gain_ref, w_bias_ref,
            pair_ref, bias_scr, bias_ref,
        )

    blocks = q_rows // ROWS
    rights, lefts = n // 2, n - 1 - n // 2
    both = min(blocks, lefts)

    def with_pair(s, carry):
        a, b = to_right(s), to_left(s)
        a.start()
        b.start()
        pair_step(s)
        a.wait()
        b.wait()
        return carry

    lax.fori_loop(0, both, with_pair, 0)
    for i in range(both, blocks):
        pair_step(i)

    heads_local = bias_out_ref.shape[1]
    copies = [
        pltpu.make_async_copy(
            bias_ref.at[pl.ds(ka * heads_local, heads_local)], bias_out_ref.at[ka], local_sem.at[1]
        )
    ]
    for d in range(1, size):
        peer = ka_peer(d)
        copies.append(
            pltpu.make_async_remote_copy(
                src_ref=bias_ref.at[pl.ds(peer * heads_local, heads_local)],
                dst_ref=bias_out_ref.at[ka],
                send_sem=bias_send.at[d - 1],
                recv_sem=bias_recv.at[d - 1],
                device_id=(pb, peer),
                device_id_type=MESH,
            )
        )
    for copy in copies:
        copy.start()

    def only_ring(s, carry):
        a, b = to_right(s), to_left(s)
        a.start()
        b.start()
        a.wait()
        b.wait()
        return carry

    if lefts > both:
        lax.fori_loop(both, lefts, only_ring, 0)
    for s in range(lefts, rights):
        last = to_right(s)
        last.start()
        last.wait()
    for copy in copies:
        copy.wait()


def pair_call(token_ids, key_cols, trunk, w_rel, cat_gain, w_in, trans_gain, ab, out, bias_gain, w_bias, kv):
    q_rows, keys, c = trunk.shape
    heads = w_bias.shape[1]
    n, size = lax.axis_size("pb"), lax.axis_size("ka")
    vmem = pl.BlockSpec(memory_space=pltpu.VMEM)
    return pl.pallas_call(
        pair_kernel,
        out_shape=(
            jax.ShapeDtypeStruct((q_rows, keys, c), BF16),
            jax.ShapeDtypeStruct((size, heads // size, q_rows, keys), BF16),
            jax.ShapeDtypeStruct((n,) + kv.shape, BF16),
        ),
        in_specs=[pl.BlockSpec(memory_space=pltpu.SMEM)] + [vmem] * 11,
        out_specs=(vmem, vmem, vmem),
        scratch_shapes=[
            pltpu.VMEM((256, c), BF16),
            pltpu.VMEM((heads, ROWS, keys), F32),
            pltpu.VMEM((heads, q_rows, keys), BF16),
            pltpu.SemaphoreType.DMA((2,)),
            pltpu.SemaphoreType.DMA((2, n // 2)),
            pltpu.SemaphoreType.DMA((2, n // 2)),
            pltpu.SemaphoreType.DMA((size - 1,)),
            pltpu.SemaphoreType.DMA((size - 1,)),
        ],
        compiler_params=pltpu.CompilerParams(
            collective_id=1, has_side_effects=True, vmem_limit_bytes=48 << 20
        ),
        cost_estimate=pl.CostEstimate(flops=2300000000, bytes_accessed=4000000, transcendentals=0),
    )(token_ids, key_cols, trunk, w_rel, cat_gain.reshape(1, -1), w_in, trans_gain, ab, out,
      bias_gain.reshape(1, -1), w_bias, kv)


def reduce_kernel(x_ref, w_ref, o_ref, part, got, send_sem, recv_sem):
    me = lax.axis_index("ka")
    pb = lax.axis_index("pb")
    size = lax.axis_size("ka")
    width = part.shape[2]
    barrier = pltpu.get_barrier_semaphore()
    for d in range(1, size):
        pl.semaphore_signal(barrier, inc=1, device_id=(pb, ka_peer(d)), device_id_type=MESH)
    whole = dot(x_ref[...], w_ref[...]).astype(BF16)
    for j in range(size):
        part[j] = whole[:, j * width : (j + 1) * width]
    pl.semaphore_wait(barrier, size - 1)
    copies = []
    for d in range(1, size):
        peer = ka_peer(d)
        copy = pltpu.make_async_remote_copy(
            src_ref=part.at[peer],
            dst_ref=got.at[d - 1],
            send_sem=send_sem.at[d - 1],
            recv_sem=recv_sem.at[d - 1],
            device_id=(pb, peer),
            device_id_type=MESH,
        )
        copy.start()
        copies.append(copy)
    total = part[me].astype(F32)
    for d, copy in enumerate(copies):
        copy.wait()
        total = total + got[d].astype(F32)
    o_ref[...] = total.astype(BF16)


def reduce_call(x, w):
    size = lax.axis_size("ka")
    rows, width = x.shape[0], w.shape[1] // size
    vmem = pl.BlockSpec(memory_space=pltpu.VMEM)
    return pl.pallas_call(
        reduce_kernel,
        out_shape=jax.ShapeDtypeStruct((rows, width), BF16),
        in_specs=[vmem, vmem],
        out_specs=vmem,
        scratch_shapes=[
            pltpu.VMEM((size, rows, width), BF16),
            pltpu.VMEM((size - 1, rows, width), BF16),
            pltpu.SemaphoreType.DMA((size - 1,)),
            pltpu.SemaphoreType.DMA((size - 1,)),
        ],
        compiler_params=pltpu.CompilerParams(
            collective_id=2, has_side_effects=True, vmem_limit_bytes=32 << 20
        ),
    )(x, w)


def soft_weights(logits):
    row_max = jnp.max(logits, axis=-1, keepdims=True)
    expweights = jnp.exp(logits - row_max)
    return (expweights / jnp.sum(expweights, axis=-1, keepdims=True)).astype(jnp.bfloat16)


def shards(
    pair_trunk,
    token_ids,
    w_rel,
    cat_gain,
    w_in,
    trans_gain,
    trans_ab,
    trans_out,
    bias_gain,
    w_bias,
    normed,
    w_proj,
    output_weight,
):
    q_rows = pair_trunk.shape[0]
    k_rows = pair_trunk.shape[1]
    k_start = lax.axis_index("ka") * k_rows
    key_ids = lax.dynamic_slice_in_dim(token_ids, k_start, k_rows, 1)
    key_cols = jnp.broadcast_to(key_ids[:, :, None], (3, k_rows, 128))
    samples = normed.shape[0]
    feat_local = normed.shape[2]
    heads_local = feat_local // HD
    ka_size = lax.axis_size("ka")
    scale_factor = 1.0 / math.sqrt(HD)
    slots = gather_call(normed)
    full = jnp.transpose(slots, (1, 2, 0, 3)).reshape(samples, q_rows, ka_size * feat_local)
    projected = jnp.einsum("sqf,pfe->psqe", full, w_proj, preferred_element_type=jnp.float32)
    kv = jnp.concatenate(
        [projected[1].astype(BF16), projected[2].astype(BF16)], axis=-1
    ).reshape(samples * q_rows, 2 * feat_local)
    pair_cond, bias_slots, kv_all = pair_call(
        token_ids, key_cols, pair_trunk, w_rel, cat_gain, w_in, trans_gain, trans_ab, trans_out,
        bias_gain, w_bias, kv,
    )
    bias_rows = jnp.transpose(bias_slots, (1, 2, 0, 3)).reshape(heads_local, q_rows, -1)
    queries = projected[0].astype(jnp.bfloat16).reshape(samples, q_rows, heads_local, HD)
    tokens = kv_all.shape[0] * q_rows
    kv_heads = kv_all.reshape(-1, samples, q_rows, 2, heads_local, HD)
    kv_heads = jnp.transpose(kv_heads, (3, 1, 4, 5, 0, 2))
    kv_heads = kv_heads.reshape(2, samples, heads_local, HD, tokens)
    keys_all, values_all = kv_heads[0], kv_heads[1]
    logits = (
        jnp.einsum("sqhd,shdk->shqk", queries, keys_all, preferred_element_type=jnp.float32)
        * scale_factor
    )
    logits = logits + bias_rows[None].astype(jnp.float32)
    weights = soft_weights(logits)
    attended = jnp.einsum(
        "shqk,shdk->sqhd", weights, values_all, preferred_element_type=jnp.float32
    )
    gated_result = (
        attended.reshape(samples, q_rows, feat_local) * jax.nn.sigmoid(projected[3])
    ).astype(jnp.bfloat16)
    update = reduce_call(gated_result.reshape(samples * q_rows, feat_local), output_weight)
    return (pair_cond, update.reshape(samples, q_rows, feat_local))


def solution(mesh):
    in_specs = (
        P("pb", "ka", None),
        P(),
        P(),
        P(),
        P(),
        P(),
        P(),
        P(),
        P(),
        P(),
        P(None, "pb", "ka"),
        P(None, None, "ka"),
        P("ka", None),
    )
    out_specs = (P("pb", "ka", None), P(None, "pb", "ka"))
    return jax.shard_map(shards, mesh=mesh, in_specs=in_specs, out_specs=out_specs, check_vma=False)
```

```python
import math
import functools

import jax
import jax.numpy as jnp
from jax import lax
from jax.experimental import pallas as pl
from jax.experimental.pallas import tpu as pltpu
from jax.sharding import PartitionSpec as P

HD = 48
RMAX = 32
SMAX = 2
REL = 139
EPS = 1e-05
F32 = jnp.float32
BF16 = jnp.bfloat16
ROWS = 16


def dot(a, b):
    return jnp.dot(a, b, preferred_element_type=F32)


def norm_rows(v, gain):
    centered = v - jnp.mean(v, axis=-1, keepdims=True)
    spread = jnp.mean(centered * centered, axis=-1, keepdims=True)
    return (centered * lax.rsqrt(spread + EPS) * gain).astype(BF16)


def onehot_row(q_res, q_chain, q_ent, q_pos, k_res, k_chain, k_ent, k_pos):
    shape = k_res.shape
    lane = lax.broadcasted_iota(jnp.int32, shape, 1)
    bins = 2 * RMAX + 2
    same_chain = k_chain == q_chain
    same_res = same_chain & (k_res == q_res)
    same_ent = k_ent == q_ent
    res_bin = jnp.where(same_chain, jnp.clip((q_res + RMAX) - k_res, 0, 2 * RMAX), bins - 1)
    tok_bin = jnp.where(
        same_res,
        jnp.clip((q_pos + (RMAX + bins)) - k_pos, bins, bins + 2 * RMAX),
        2 * bins - 1,
    )
    chain_bin = jnp.where(
        same_ent,
        jnp.clip((q_chain + (SMAX + 2 * bins)) - k_chain, 2 * bins, 2 * bins + 2 * SMAX),
        2 * bins + 2 * SMAX + 1,
    )
    low = (lane == res_bin) | (lane == tok_bin)
    high_lane = lane + 128
    high = (high_lane == tok_bin) | (high_lane == chain_bin)
    high = high | ((high_lane == REL - 1) & same_ent)
    one = jnp.where(low, 1.0, 0.0)
    two = jnp.where(high, 1.0, 0.0)
    return jnp.concatenate([one, two], axis=-1).astype(BF16)


def pair_block(
    begin,
    q_start,
    k_pos,
    tok_ref,
    key_ref,
    trunk_ref,
    wrel_scr,
    cat_gain_ref,
    w_in_ref,
    trans_gain_ref,
    ab_ref,
    out_ref,
    bias_gain_ref,
    w_bias_ref,
    pair_ref,
    bias_scr,
    bias_ref,
):
    keys = trunk_ref.shape[1]
    c = trunk_ref.shape[2]
    k_res, k_chain, k_ent = key_ref[0], key_ref[1], key_ref[2]
    rows = []
    for r in range(ROWS):
        at = q_start + begin + r
        rows.append(
            onehot_row(
                tok_ref[0, at], tok_ref[1, at], tok_ref[2, at], at, k_res, k_chain, k_ent, k_pos
            )
        )
    onehot = jnp.concatenate(rows, axis=0)
    rel = dot(onehot, wrel_scr[...])
    trunk = trunk_ref[pl.ds(begin, ROWS)].reshape(ROWS * keys, c).astype(F32)
    mean = jnp.sum(trunk + rel, axis=-1, keepdims=True) * (1.0 / (2 * c))
    ct = trunk - mean
    cr = rel - mean
    var = jnp.sum(ct * ct + cr * cr, axis=-1, keepdims=True) * (1.0 / (2 * c))
    inv = lax.rsqrt(var + EPS)
    gain = cat_gain_ref[...]
    normal_in = jnp.concatenate(
        [(ct * inv * gain[:, :c]).astype(BF16), (cr * inv * gain[:, c:]).astype(BF16)], axis=-1
    )
    state = dot(normal_in, w_in_ref[...])
    half = out_ref.shape[1]
    for l in range(2):
        normal = norm_rows(state, trans_gain_ref[l : l + 1, :])
        gate_up = dot(normal, ab_ref[l])
        gate_half = gate_up[:, :half] * 0.5
        silu = gate_half + gate_half * jnp.tanh(gate_half)
        hidden = (silu * gate_up[:, half:]).astype(BF16)
        state = state + dot(hidden, out_ref[l])
    pair_ref[pl.ds(begin, ROWS)] = state.astype(BF16).reshape(ROWS, keys, c)
    normal_b = norm_rows(state, bias_gain_ref[...])
    for r in range(ROWS):
        bias_scr[:, r, :] = lax.dot_general(
            w_bias_ref[...],
            normal_b[r * keys : (r + 1) * keys],
            (((0,), (1,)), ((), ())),
            preferred_element_type=F32,
        )
    bias_ref[:, pl.ds(begin, ROWS), :] = bias_scr[...].astype(BF16)


MESH = pl.DeviceIdType.MESH


def ka_peer(offset):
    size = lax.axis_size("ka")
    return lax.rem(lax.axis_index("ka") + offset, size)


def ring_index(pos):
    n = lax.axis_size("pb")
    pos = lax.rem(pos + 2 * n, n)
    if n % 2:
        return pos
    return jnp.where(pos < n // 2, 2 * pos, 2 * (n - 1 - pos) + 1)


def ring_position(index):
    n = lax.axis_size("pb")
    if n % 2:
        return index
    half = index // 2
    return jnp.where(lax.rem(index, 2) == 0, half, n - 1 - half)


def pad128(v):
    return -(-v // 128) * 128


def gather_kernel(x_ref, w_ref, q_ref, kv_ref, gate_ref, got, send_sem, recv_sem):
    me = lax.axis_index("ka")
    pb = lax.axis_index("pb")
    size = lax.axis_size("ka")
    samples, q_rows, feat = x_ref.shape
    barrier = pltpu.get_barrier_semaphore()
    for d in range(1, size):
        pl.semaphore_signal(barrier, inc=1, device_id=(pb, ka_peer(d)), device_id_type=MESH)
    pl.semaphore_wait(barrier, size - 1)
    copies = []
    for d in range(1, size):
        copy = pltpu.make_async_remote_copy(
            src_ref=x_ref,
            dst_ref=got.at[d - 1],
            send_sem=send_sem.at[d - 1],
            recv_sem=recv_sem.at[d - 1],
            device_id=(pb, ka_peer(d)),
            device_id_type=MESH,
        )
        copy.start()
        copies.append(copy)

    def part(x, owner):
        rows = pl.ds(pl.multiple_of(owner * feat, 16), feat)
        x = x.reshape(samples * q_rows, feat)
        return [dot(x, w_ref[p, rows, :]) for p in range(4)]

    sums = part(x_ref[...], me)
    for d in range(1, size):
        copies[d - 1].wait()
        more = part(got[d - 1], ka_peer(size - d))
        sums = [u + v for u, v in zip(sums, more)]
    q_ref[...] = jnp.zeros_like(q_ref)
    q_ref[:, :feat] = sums[0].astype(BF16)
    kv_ref[:, :feat] = sums[1].astype(BF16)
    kv_ref[:, feat:] = sums[2].astype(BF16)
    gate_ref[...] = sums[3]


def gather_call(x, w_proj):
    size = lax.axis_size("ka")
    samples, q_rows, feat = x.shape
    rows = samples * q_rows
    vmem = pl.BlockSpec(memory_space=pltpu.VMEM)
    return pl.pallas_call(
        gather_kernel,
        out_shape=(
            jax.ShapeDtypeStruct((rows, min(2 * feat, pad128(feat))), BF16),
            jax.ShapeDtypeStruct((rows, 2 * feat), BF16),
            jax.ShapeDtypeStruct((rows, feat), F32),
        ),
        in_specs=[vmem, vmem],
        out_specs=(vmem, vmem, vmem),
        scratch_shapes=[
            pltpu.VMEM((size - 1,) + x.shape, BF16),
            pltpu.SemaphoreType.DMA((size - 1,)),
            pltpu.SemaphoreType.DMA((size - 1,)),
        ],
        compiler_params=pltpu.CompilerParams(
            collective_id=0, has_side_effects=True, vmem_limit_bytes=24 << 20
        ),
    )(x, w_proj)


def pair_kernel(
    tok_ref, *refs
):
    sources, refs = refs[:10], refs[10:]
    kv_ref, pair_ref, bias_out_ref, kv_out_ref = refs[:4]
    wrel_scr, bias_scr, bias_ref, local_sem, ring_send, ring_recv, bias_send, bias_recv = refs[4:12]
    fetch_sem, held = refs[12], refs[13:]
    fetches = [
        pltpu.make_async_copy(src, dst, fetch_sem.at[i])
        for i, (src, dst) in enumerate(zip(sources, held))
    ]
    for fetch in fetches:
        fetch.start()
    (key_ref, trunk_ref, w_rel_ref, cat_gain_ref, w_in_ref, trans_gain_ref, ab_ref, out_ref,
     bias_gain_ref, w_bias_ref) = held
    q_rows, keys = trunk_ref.shape[0], trunk_ref.shape[1]
    n = lax.axis_size("pb")
    size = lax.axis_size("ka")
    pb = lax.axis_index("pb")
    ka = lax.axis_index("ka")
    pos = ring_position(pb)
    right, left = ring_index(pos + 1), ring_index(pos + n - 1)

    barrier = pltpu.get_barrier_semaphore()
    for side in (left, right):
        pl.semaphore_signal(barrier, inc=1, device_id=(side, ka), device_id_type=MESH)
    for d in range(1, size):
        pl.semaphore_signal(barrier, inc=1, device_id=(pb, ka_peer(d)), device_id_type=MESH)
    own = pltpu.make_async_copy(kv_ref, kv_out_ref.at[pb], local_sem.at[0])
    own.start()
    own.wait()
    for fetch in fetches:
        fetch.wait()

    q_start = pb * q_rows
    k_start = ka * keys
    wrel_scr[...] = jnp.zeros_like(wrel_scr)
    wrel_scr[0:REL, :] = w_rel_ref[...]
    k_pos = k_start + lax.broadcasted_iota(jnp.int32, key_ref.shape[1:], 0)
    pl.semaphore_wait(barrier, 2 + size - 1)

    def to_right(s):
        slot = kv_out_ref.at[ring_index(pos + n - s)]
        return pltpu.make_async_remote_copy(
            src_ref=slot, dst_ref=slot, send_sem=ring_send.at[0, s], recv_sem=ring_recv.at[0, s],
            device_id=(right, ka), device_id_type=MESH,
        )

    def to_left(s):
        slot = kv_out_ref.at[ring_index(pos + s)]
        return pltpu.make_async_remote_copy(
            src_ref=slot, dst_ref=slot, send_sem=ring_send.at[1, s], recv_sem=ring_recv.at[1, s],
            device_id=(left, ka), device_id_type=MESH,
        )

    def pair_step(i):
        pair_block(
            pl.multiple_of(i * ROWS, ROWS), q_start, k_pos, tok_ref, key_ref, trunk_ref, wrel_scr,
            cat_gain_ref, w_in_ref, trans_gain_ref, ab_ref, out_ref, bias_gain_ref, w_bias_ref,
            pair_ref, bias_scr, bias_ref,
        )

    blocks = q_rows // ROWS
    rights, lefts = n // 2, n - 1 - n // 2
    both = min(blocks, lefts)

    def with_pair(s, carry):
        a, b = to_right(s), to_left(s)
        a.start()
        b.start()
        pair_step(s)
        a.wait()
        b.wait()
        return carry

    lax.fori_loop(0, both, with_pair, 0)
    for i in range(both, blocks):
        pair_step(i)

    heads_local = bias_out_ref.shape[1]
    copies = [
        pltpu.make_async_copy(
            bias_ref.at[pl.ds(ka * heads_local, heads_local)], bias_out_ref.at[ka], local_sem.at[1]
        )
    ]
    for d in range(1, size):
        peer = ka_peer(d)
        copies.append(
            pltpu.make_async_remote_copy(
                src_ref=bias_ref.at[pl.ds(peer * heads_local, heads_local)],
                dst_ref=bias_out_ref.at[ka],
                send_sem=bias_send.at[d - 1],
                recv_sem=bias_recv.at[d - 1],
                device_id=(pb, peer),
                device_id_type=MESH,
            )
        )
    for copy in copies:
        copy.start()

    def only_ring(s, carry):
        a, b = to_right(s), to_left(s)
        a.start()
        b.start()
        a.wait()
        b.wait()
        return carry

    if lefts > both:
        lax.fori_loop(both, lefts, only_ring, 0)
    for s in range(lefts, rights):
        last = to_right(s)
        last.start()
        last.wait()
    for copy in copies:
        copy.wait()


def pair_call(token_ids, key_cols, trunk, w_rel, cat_gain, w_in, trans_gain, ab, out, bias_gain, w_bias, kv):
    q_rows, keys, c = trunk.shape
    heads = w_bias.shape[1]
    n, size = lax.axis_size("pb"), lax.axis_size("ka")
    vmem = pl.BlockSpec(memory_space=pltpu.VMEM)
    fetched = (key_cols, trunk, w_rel, cat_gain.reshape(1, -1), w_in, trans_gain, ab, out,
               bias_gain.reshape(1, -1), w_bias)
    hbm = pl.BlockSpec(memory_space=pltpu.HBM)
    return pl.pallas_call(
        pair_kernel,
        out_shape=(
            jax.ShapeDtypeStruct((q_rows, keys, c), BF16),
            jax.ShapeDtypeStruct((size, heads // size, q_rows, keys), BF16),
            jax.ShapeDtypeStruct((n,) + kv.shape, BF16),
        ),
        in_specs=[pl.BlockSpec(memory_space=pltpu.SMEM)] + [hbm] * 10 + [vmem],
        out_specs=(vmem, vmem, vmem),
        scratch_shapes=[
            pltpu.VMEM((256, c), BF16),
            pltpu.VMEM((heads, ROWS, keys), F32),
            pltpu.VMEM((heads, q_rows, keys), BF16),
            pltpu.SemaphoreType.DMA((2,)),
            pltpu.SemaphoreType.DMA((2, n // 2)),
            pltpu.SemaphoreType.DMA((2, n // 2)),
            pltpu.SemaphoreType.DMA((size - 1,)),
            pltpu.SemaphoreType.DMA((size - 1,)),
            pltpu.SemaphoreType.DMA((10,)),
        ] + [pltpu.VMEM(v.shape, v.dtype) for v in fetched],
        compiler_params=pltpu.CompilerParams(
            collective_id=1, has_side_effects=True, vmem_limit_bytes=48 << 20
        ),
        cost_estimate=pl.CostEstimate(flops=2300000000, bytes_accessed=4000000, transcendentals=0),
    )(token_ids, *fetched, kv)


def attend_sample(s, q_rows, q_ref, kv_ref, gate_ref, bias_scr, gated):
    feat = gate_ref.shape[1]
    heads = feat // HD
    wide = q_ref.shape[1]
    low = feat // 128 * 128
    off = feat - low
    tokens = kv_ref.shape[0] * q_rows
    rows = pl.ds(pl.multiple_of(s * q_rows, 16), q_rows)
    q = q_ref[rows, :].astype(F32)
    lane = lax.broadcasted_iota(jnp.int32, q.shape, 1)
    q_heads = jnp.concatenate(
        [
            jnp.where((lane >= h * HD) & (lane < (h + 1) * HD), q, 0.0).astype(BF16)
            for h in range(heads)
        ],
        axis=0,
    )
    keys = kv_ref[:, rows, :wide].reshape(tokens, wide)
    values = kv_ref[:, rows, low:].reshape(tokens, 2 * feat - low)
    logits = lax.dot_general(
        q_heads, keys, (((1,), (1,)), ((), ())), preferred_element_type=F32
    )
    logits = logits * (1.0 / math.sqrt(HD)) + bias_scr[...]
    top = jnp.max(logits, axis=-1, keepdims=True)
    powers = jnp.exp(logits - top)
    inv = 1.0 / jnp.sum(powers, axis=-1, keepdims=True)
    mixed = dot((powers * inv).astype(BF16), values)
    lane = lax.broadcasted_iota(jnp.int32, (q_rows, 2 * feat - low), 1) - off
    attended = jnp.zeros((q_rows, 2 * feat - low), F32)
    for h in range(heads):
        mine = mixed[h * q_rows : (h + 1) * q_rows]
        attended = jnp.where((lane >= h * HD) & (lane < (h + 1) * HD), mine, attended)
    gate = 0.5 + 0.5 * jnp.tanh(0.5 * gate_ref[rows, :])
    gated[rows, :] = (attended[:, off:] * gate).astype(BF16)


def reduce_kernel(
    q_ref, kv_ref, gate_ref, bias_ref, w_ref, o_ref, bias_scr, gated, part, got, send_sem, recv_sem
):
    me = lax.axis_index("ka")
    pb = lax.axis_index("pb")
    size = lax.axis_size("ka")
    width = part.shape[2]
    barrier = pltpu.get_barrier_semaphore()
    for d in range(1, size):
        pl.semaphore_signal(barrier, inc=1, device_id=(pb, ka_peer(d)), device_id_type=MESH)
    keys = bias_ref.shape[3]
    q_rows = bias_ref.shape[2]
    for j in range(size):
        bias_scr[:, j * keys : (j + 1) * keys] = (
            bias_ref[j].reshape(bias_scr.shape[0], keys).astype(F32)
        )

    def step(i, carry):
        for u in range(2):
            attend_sample(2 * i + u, q_rows, q_ref, kv_ref, gate_ref, bias_scr, gated)
        return carry

    lax.fori_loop(0, gated.shape[0] // (2 * q_rows), step, 0)
    whole = dot(gated[...], w_ref[...]).astype(BF16)
    for j in range(size):
        part[j] = whole[:, j * width : (j + 1) * width]
    pl.semaphore_wait(barrier, size - 1)
    copies = []
    for d in range(1, size):
        peer = ka_peer(d)
        copy = pltpu.make_async_remote_copy(
            src_ref=part.at[peer],
            dst_ref=got.at[d - 1],
            send_sem=send_sem.at[d - 1],
            recv_sem=recv_sem.at[d - 1],
            device_id=(pb, peer),
            device_id_type=MESH,
        )
        copy.start()
        copies.append(copy)
    total = part[me].astype(F32)
    for d, copy in enumerate(copies):
        copy.wait()
        total = total + got[d].astype(F32)
    o_ref[...] = total.astype(BF16)


def reduce_call(q, kv_all, gate, bias_slots, w):
    size = lax.axis_size("ka")
    rows, width = gate.shape[0], w.shape[1] // size
    heads, q_rows, keys = bias_slots.shape[1:]
    vmem = pl.BlockSpec(memory_space=pltpu.VMEM)
    return pl.pallas_call(
        reduce_kernel,
        out_shape=jax.ShapeDtypeStruct((rows, width), BF16),
        in_specs=[vmem] * 5,
        out_specs=vmem,
        scratch_shapes=[
            pltpu.VMEM((heads * q_rows, size * keys), F32),
            pltpu.VMEM(gate.shape, BF16),
            pltpu.VMEM((size, rows, width), BF16),
            pltpu.VMEM((size - 1, rows, width), BF16),
            pltpu.SemaphoreType.DMA((size - 1,)),
            pltpu.SemaphoreType.DMA((size - 1,)),
        ],
        compiler_params=pltpu.CompilerParams(
            collective_id=2, has_side_effects=True, vmem_limit_bytes=32 << 20
        ),
    )(q, kv_all, gate, bias_slots, w)


def shards(
    pair_trunk,
    token_ids,
    w_rel,
    cat_gain,
    w_in,
    trans_gain,
    trans_ab,
    trans_out,
    bias_gain,
    w_bias,
    normed,
    w_proj,
    output_weight,
):
    q_rows = pair_trunk.shape[0]
    k_rows = pair_trunk.shape[1]
    k_start = lax.axis_index("ka") * k_rows
    key_ids = lax.dynamic_slice_in_dim(token_ids, k_start, k_rows, 1)
    key_cols = jnp.broadcast_to(key_ids[:, :, None], (3, k_rows, 128))
    samples = normed.shape[0]
    feat_local = normed.shape[2]
    q, kv, gate = gather_call(normed, w_proj)
    pair_cond, bias_slots, kv_all = pair_call(
        token_ids, key_cols, pair_trunk, w_rel, cat_gain, w_in, trans_gain, trans_ab, trans_out,
        bias_gain, w_bias, kv,
    )
    update = reduce_call(q, kv_all, gate, bias_slots, output_weight)
    return (pair_cond, update.reshape(samples, q_rows, feat_local))


def solution(mesh):
    in_specs = (
        P("pb", "ka", None),
        P(),
        P(),
        P(),
        P(),
        P(),
        P(),
        P(),
        P(),
        P(),
        P(None, "pb", "ka"),
        P(None, None, "ka"),
        P("ka", None),
    )
    out_specs = (P("pb", "ka", None), P(None, "pb", "ka"))
    return jax.shard_map(shards, mesh=mesh, in_specs=in_specs, out_specs=out_specs, check_vma=False)
```

```python
import math
import functools

import jax
import jax.numpy as jnp
from jax import lax
from jax.experimental import pallas as pl
from jax.experimental.pallas import tpu as pltpu
from jax.sharding import PartitionSpec as P

HD = 48
RMAX = 32
SMAX = 2
REL = 139
EPS = 1e-05
F32 = jnp.float32
BF16 = jnp.bfloat16
ROWS = 16


def dot(a, b):
    return jnp.dot(a, b, preferred_element_type=F32)


def norm_rows(v, gain):
    centered = v - jnp.mean(v, axis=-1, keepdims=True)
    spread = jnp.mean(centered * centered, axis=-1, keepdims=True)
    return (centered * lax.rsqrt(spread + EPS) * gain).astype(BF16)


def onehot_row(q_res, q_chain, q_ent, q_pos, k_res, k_chain, k_ent, k_pos):
    shape = k_res.shape
    lane = lax.broadcasted_iota(jnp.int32, shape, 1)
    bins = 2 * RMAX + 2
    same_chain = k_chain == q_chain
    same_res = same_chain & (k_res == q_res)
    same_ent = k_ent == q_ent
    res_bin = jnp.where(same_chain, jnp.clip((q_res + RMAX) - k_res, 0, 2 * RMAX), bins - 1)
    tok_bin = jnp.where(
        same_res,
        jnp.clip((q_pos + (RMAX + bins)) - k_pos, bins, bins + 2 * RMAX),
        2 * bins - 1,
    )
    chain_bin = jnp.where(
        same_ent,
        jnp.clip((q_chain + (SMAX + 2 * bins)) - k_chain, 2 * bins, 2 * bins + 2 * SMAX),
        2 * bins + 2 * SMAX + 1,
    )
    low = (lane == res_bin) | (lane == tok_bin)
    high_lane = lane + 128
    high = (high_lane == tok_bin) | (high_lane == chain_bin)
    high = high | ((high_lane == REL - 1) & same_ent)
    one = jnp.where(low, 1.0, 0.0)
    two = jnp.where(high, 1.0, 0.0)
    return jnp.concatenate([one, two], axis=-1).astype(BF16)


def pair_block(
    begin,
    q_start,
    k_pos,
    tok_ref,
    key_ref,
    trunk_ref,
    wrel_scr,
    cat_gain_ref,
    w_in_ref,
    trans_gain_ref,
    ab_ref,
    out_ref,
    bias_gain_ref,
    w_bias_ref,
    pair_ref,
    bias_scr,
    bias_ref,
):
    keys = trunk_ref.shape[1]
    c = trunk_ref.shape[2]
    k_res, k_chain, k_ent = key_ref[0], key_ref[1], key_ref[2]
    rows = []
    for r in range(ROWS):
        at = q_start + begin + r
        rows.append(
            onehot_row(
                tok_ref[0, at], tok_ref[1, at], tok_ref[2, at], at, k_res, k_chain, k_ent, k_pos
            )
        )
    onehot = jnp.concatenate(rows, axis=0)
    rel = dot(onehot, wrel_scr[...])
    trunk = trunk_ref[pl.ds(begin, ROWS)].reshape(ROWS * keys, c).astype(F32)
    mean = jnp.sum(trunk + rel, axis=-1, keepdims=True) * (1.0 / (2 * c))
    ct = trunk - mean
    cr = rel - mean
    var = jnp.sum(ct * ct + cr * cr, axis=-1, keepdims=True) * (1.0 / (2 * c))
    inv = lax.rsqrt(var + EPS)
    gain = cat_gain_ref[...]
    normal_in = jnp.concatenate(
        [(ct * inv * gain[:, :c]).astype(BF16), (cr * inv * gain[:, c:]).astype(BF16)], axis=-1
    )
    state = dot(normal_in, w_in_ref[...])
    half = out_ref.shape[1]
    for l in range(2):
        normal = norm_rows(state, trans_gain_ref[l : l + 1, :])
        gate_up = dot(normal, ab_ref[l])
        gate_half = gate_up[:, :half] * 0.5
        silu = gate_half + gate_half * jnp.tanh(gate_half)
        hidden = (silu * gate_up[:, half:]).astype(BF16)
        state = state + dot(hidden, out_ref[l])
    pair_ref[pl.ds(begin, ROWS)] = state.astype(BF16).reshape(ROWS, keys, c)
    normal_b = norm_rows(state, bias_gain_ref[...])
    for r in range(ROWS):
        bias_scr[:, r, :] = lax.dot_general(
            w_bias_ref[...],
            normal_b[r * keys : (r + 1) * keys],
            (((0,), (1,)), ((), ())),
            preferred_element_type=F32,
        )
    bias_ref[:, pl.ds(begin, ROWS), :] = bias_scr[...].astype(BF16)


MESH = pl.DeviceIdType.MESH


def ka_peer(offset):
    size = lax.axis_size("ka")
    return lax.rem(lax.axis_index("ka") + offset, size)


def ring_index(pos):
    n = lax.axis_size("pb")
    pos = lax.rem(pos + 2 * n, n)
    if n % 2:
        return pos
    return jnp.where(pos < n // 2, 2 * pos, 2 * (n - 1 - pos) + 1)


def ring_position(index):
    n = lax.axis_size("pb")
    if n % 2:
        return index
    half = index // 2
    return jnp.where(lax.rem(index, 2) == 0, half, n - 1 - half)


def pad128(v):
    return -(-v // 128) * 128


def gather_kernel(x_ref, w_ref, q_ref, kv_ref, gate_ref, got, send_sem, recv_sem):
    me = lax.axis_index("ka")
    pb = lax.axis_index("pb")
    size = lax.axis_size("ka")
    samples, q_rows, feat = x_ref.shape
    barrier = pltpu.get_barrier_semaphore()
    for d in range(1, size):
        pl.semaphore_signal(barrier, inc=1, device_id=(pb, ka_peer(d)), device_id_type=MESH)
    pl.semaphore_wait(barrier, size - 1)
    copies = []
    for d in range(1, size):
        copy = pltpu.make_async_remote_copy(
            src_ref=x_ref,
            dst_ref=got.at[d - 1],
            send_sem=send_sem.at[d - 1],
            recv_sem=recv_sem.at[d - 1],
            device_id=(pb, ka_peer(d)),
            device_id_type=MESH,
        )
        copy.start()
        copies.append(copy)

    def part(x, owner):
        rows = pl.ds(pl.multiple_of(owner * feat, 16), feat)
        x = x.reshape(samples * q_rows, feat)
        return [dot(x, w_ref[p, rows, :]) for p in range(4)]

    sums = part(x_ref[...], me)
    for d in range(1, size):
        copies[d - 1].wait()
        more = part(got[d - 1], ka_peer(size - d))
        sums = [u + v for u, v in zip(sums, more)]
    q_ref[...] = jnp.zeros_like(q_ref)
    q_ref[:, :feat] = sums[0].astype(BF16)
    kv_ref[:, :feat] = sums[1].astype(BF16)
    kv_ref[:, feat:] = sums[2].astype(BF16)
    gate_ref[...] = sums[3]


def gather_call(x, w_proj):
    size = lax.axis_size("ka")
    samples, q_rows, feat = x.shape
    rows = samples * q_rows
    vmem = pl.BlockSpec(memory_space=pltpu.VMEM)
    return pl.pallas_call(
        gather_kernel,
        out_shape=(
            jax.ShapeDtypeStruct((rows, min(2 * feat, pad128(feat))), BF16),
            jax.ShapeDtypeStruct((rows, 2 * feat), BF16),
            jax.ShapeDtypeStruct((rows, feat), F32),
        ),
        in_specs=[vmem, vmem],
        out_specs=(vmem, vmem, vmem),
        scratch_shapes=[
            pltpu.VMEM((size - 1,) + x.shape, BF16),
            pltpu.SemaphoreType.DMA((size - 1,)),
            pltpu.SemaphoreType.DMA((size - 1,)),
        ],
        compiler_params=pltpu.CompilerParams(
            collective_id=0, has_side_effects=True, vmem_limit_bytes=24 << 20
        ),
    )(x, w_proj)


def pair_kernel(
    tok_ref, *refs
):
    sources, refs = refs[:10], refs[10:]
    kv_ref, pair_ref, bias_out_ref, kv_out_ref = refs[:4]
    wrel_scr, bias_scr, bias_ref, local_sem, ring_send, ring_recv, bias_send, bias_recv = refs[4:12]
    fetch_sem, held = refs[12], refs[13:]
    fetches = [
        pltpu.make_async_copy(src, dst, fetch_sem.at[i])
        for i, (src, dst) in enumerate(zip(sources, held))
    ]
    for fetch in fetches:
        fetch.start()
    (key_ref, trunk_ref, w_rel_ref, cat_gain_ref, w_in_ref, trans_gain_ref, ab_ref, out_ref,
     bias_gain_ref, w_bias_ref) = held
    q_rows, keys = trunk_ref.shape[0], trunk_ref.shape[1]
    n = lax.axis_size("pb")
    size = lax.axis_size("ka")
    pb = lax.axis_index("pb")
    ka = lax.axis_index("ka")
    pos = ring_position(pb)
    right, left = ring_index(pos + 1), ring_index(pos + n - 1)

    barrier = pltpu.get_barrier_semaphore()
    for side in (left, right):
        pl.semaphore_signal(barrier, inc=1, device_id=(side, ka), device_id_type=MESH)
    for d in range(1, size):
        pl.semaphore_signal(barrier, inc=1, device_id=(pb, ka_peer(d)), device_id_type=MESH)
    own = pltpu.make_async_copy(kv_ref, kv_out_ref.at[pb], local_sem.at[0])
    own.start()
    own.wait()
    for fetch in fetches:
        fetch.wait()

    q_start = pb * q_rows
    k_start = ka * keys
    wrel_scr[...] = jnp.zeros_like(wrel_scr)
    wrel_scr[0:REL, :] = w_rel_ref[...]
    k_pos = k_start + lax.broadcasted_iota(jnp.int32, key_ref.shape[1:], 0)
    pl.semaphore_wait(barrier, 2 + size - 1)

    half = kv_ref.shape[0] // 2

    def hop(way, s, c):
        owner = ring_index(pos + n - s) if way == 0 else ring_index(pos + s)
        piece = kv_out_ref.at[owner, pl.ds(c * half, half)]
        return pltpu.make_async_remote_copy(
            src_ref=piece,
            dst_ref=piece,
            send_sem=ring_send.at[way, c, s],
            recv_sem=ring_recv.at[way, c, s],
            device_id=(right if way == 0 else left, ka),
            device_id_type=MESH,
        )

    def pair_step(i):
        pair_block(
            pl.multiple_of(i * ROWS, ROWS), q_start, k_pos, tok_ref, key_ref, trunk_ref, wrel_scr,
            cat_gain_ref, w_in_ref, trans_gain_ref, ab_ref, out_ref, bias_gain_ref, w_bias_ref,
            pair_ref, bias_scr, bias_ref,
        )

    blocks = q_rows // ROWS
    even = n % 2 == 0
    full = n - 1 - n // 2
    both = min(blocks, full)

    for c in range(2):
        for way in range(2):
            hop(way, 0, c).start()

    def advance(s):
        for c in range(2):
            for way in range(2):
                hop(way, s, c).wait_recv()
                if even and way == c:
                    hop(way, s + 1, c).start()
                else:

                    @pl.when(s + 1 < full)
                    def _():
                        hop(way, s + 1, c).start()

    def with_pair(s, carry):
        pair_step(s)
        advance(s)
        return carry

    def only_ring(s, carry):
        advance(s)
        return carry

    lax.fori_loop(0, both, with_pair, 0)
    for i in range(both, blocks):
        pair_step(i)

    heads_local = bias_out_ref.shape[1]
    copies = [
        pltpu.make_async_copy(
            bias_ref.at[pl.ds(ka * heads_local, heads_local)], bias_out_ref.at[ka], local_sem.at[1]
        )
    ]
    for d in range(1, size):
        peer = ka_peer(d)
        copies.append(
            pltpu.make_async_remote_copy(
                src_ref=bias_ref.at[pl.ds(peer * heads_local, heads_local)],
                dst_ref=bias_out_ref.at[ka],
                send_sem=bias_send.at[d - 1],
                recv_sem=bias_recv.at[d - 1],
                device_id=(pb, peer),
                device_id_type=MESH,
            )
        )
    for copy in copies:
        copy.start()

    if full > both:
        lax.fori_loop(both, full, only_ring, 0)
    if even:
        hop(0, full, 0).wait()
        hop(1, full, 1).wait()

    def drain(s, carry):
        for c in range(2):
            for way in range(2):
                hop(way, s, c).wait_send()
        return carry

    lax.fori_loop(0, full, drain, 0)
    for copy in copies:
        copy.wait()


def pair_call(token_ids, key_cols, trunk, w_rel, cat_gain, w_in, trans_gain, ab, out, bias_gain, w_bias, kv):
    q_rows, keys, c = trunk.shape
    heads = w_bias.shape[1]
    n, size = lax.axis_size("pb"), lax.axis_size("ka")
    vmem = pl.BlockSpec(memory_space=pltpu.VMEM)
    fetched = (key_cols, trunk, w_rel, cat_gain.reshape(1, -1), w_in, trans_gain, ab, out,
               bias_gain.reshape(1, -1), w_bias)
    hbm = pl.BlockSpec(memory_space=pltpu.HBM)
    return pl.pallas_call(
        pair_kernel,
        out_shape=(
            jax.ShapeDtypeStruct((q_rows, keys, c), BF16),
            jax.ShapeDtypeStruct((size, heads // size, q_rows, keys), BF16),
            jax.ShapeDtypeStruct((n,) + kv.shape, BF16),
        ),
        in_specs=[pl.BlockSpec(memory_space=pltpu.SMEM)] + [hbm] * 10 + [vmem],
        out_specs=(vmem, vmem, vmem),
        scratch_shapes=[
            pltpu.VMEM((256, c), BF16),
            pltpu.VMEM((heads, ROWS, keys), F32),
            pltpu.VMEM((heads, q_rows, keys), BF16),
            pltpu.SemaphoreType.DMA((2,)),
            pltpu.SemaphoreType.DMA((2, 2, n // 2)),
            pltpu.SemaphoreType.DMA((2, 2, n // 2)),
            pltpu.SemaphoreType.DMA((size - 1,)),
            pltpu.SemaphoreType.DMA((size - 1,)),
            pltpu.SemaphoreType.DMA((10,)),
        ] + [pltpu.VMEM(v.shape, v.dtype) for v in fetched],
        compiler_params=pltpu.CompilerParams(
            collective_id=1, has_side_effects=True, vmem_limit_bytes=48 << 20
        ),
        cost_estimate=pl.CostEstimate(flops=2300000000, bytes_accessed=4000000, transcendentals=0),
    )(token_ids, *fetched, kv)


def attend_sample(s, q_rows, q_ref, kv_ref, gate_ref, bias_scr, gated):
    feat = gate_ref.shape[1]
    heads = feat // HD
    wide = q_ref.shape[1]
    low = feat // 128 * 128
    off = feat - low
    tokens = kv_ref.shape[0] * q_rows
    rows = pl.ds(pl.multiple_of(s * q_rows, 16), q_rows)
    q = q_ref[rows, :].astype(F32)
    lane = lax.broadcasted_iota(jnp.int32, q.shape, 1)
    q_heads = jnp.concatenate(
        [
            jnp.where((lane >= h * HD) & (lane < (h + 1) * HD), q, 0.0).astype(BF16)
            for h in range(heads)
        ],
        axis=0,
    )
    keys = kv_ref[:, rows, :wide].reshape(tokens, wide)
    values = kv_ref[:, rows, low:].reshape(tokens, 2 * feat - low)
    logits = lax.dot_general(
        q_heads, keys, (((1,), (1,)), ((), ())), preferred_element_type=F32
    )
    logits = logits * (1.0 / math.sqrt(HD)) + bias_scr[...]
    top = jnp.max(logits, axis=-1, keepdims=True)
    powers = jnp.exp(logits - top)
    inv = 1.0 / jnp.sum(powers, axis=-1, keepdims=True)
    mixed = dot((powers * inv).astype(BF16), values)
    lane = lax.broadcasted_iota(jnp.int32, (q_rows, 2 * feat - low), 1) - off
    attended = jnp.zeros((q_rows, 2 * feat - low), F32)
    for h in range(heads):
        mine = mixed[h * q_rows : (h + 1) * q_rows]
        attended = jnp.where((lane >= h * HD) & (lane < (h + 1) * HD), mine, attended)
    gate = 0.5 + 0.5 * jnp.tanh(0.5 * gate_ref[rows, :])
    gated[rows, :] = (attended[:, off:] * gate).astype(BF16)


def reduce_kernel(
    q_ref, kv_ref, gate_ref, bias_ref, w_ref, o_ref, bias_scr, gated, part, got, send_sem, recv_sem
):
    me = lax.axis_index("ka")
    pb = lax.axis_index("pb")
    size = lax.axis_size("ka")
    width = part.shape[2]
    barrier = pltpu.get_barrier_semaphore()
    for d in range(1, size):
        pl.semaphore_signal(barrier, inc=1, device_id=(pb, ka_peer(d)), device_id_type=MESH)
    keys = bias_ref.shape[3]
    q_rows = bias_ref.shape[2]
    for j in range(size):
        bias_scr[:, j * keys : (j + 1) * keys] = (
            bias_ref[j].reshape(bias_scr.shape[0], keys).astype(F32)
        )

    def step(i, carry):
        for u in range(2):
            attend_sample(2 * i + u, q_rows, q_ref, kv_ref, gate_ref, bias_scr, gated)
        return carry

    lax.fori_loop(0, gated.shape[0] // (2 * q_rows), step, 0)
    whole = dot(gated[...], w_ref[...]).astype(BF16)
    for j in range(size):
        part[j] = whole[:, j * width : (j + 1) * width]
    pl.semaphore_wait(barrier, size - 1)
    copies = []
    for d in range(1, size):
        peer = ka_peer(d)
        copy = pltpu.make_async_remote_copy(
            src_ref=part.at[peer],
            dst_ref=got.at[d - 1],
            send_sem=send_sem.at[d - 1],
            recv_sem=recv_sem.at[d - 1],
            device_id=(pb, peer),
            device_id_type=MESH,
        )
        copy.start()
        copies.append(copy)
    total = part[me].astype(F32)
    for d, copy in enumerate(copies):
        copy.wait()
        total = total + got[d].astype(F32)
    o_ref[...] = total.astype(BF16)


def reduce_call(q, kv_all, gate, bias_slots, w):
    size = lax.axis_size("ka")
    rows, width = gate.shape[0], w.shape[1] // size
    heads, q_rows, keys = bias_slots.shape[1:]
    vmem = pl.BlockSpec(memory_space=pltpu.VMEM)
    return pl.pallas_call(
        reduce_kernel,
        out_shape=jax.ShapeDtypeStruct((rows, width), BF16),
        in_specs=[vmem] * 5,
        out_specs=vmem,
        scratch_shapes=[
            pltpu.VMEM((heads * q_rows, size * keys), F32),
            pltpu.VMEM(gate.shape, BF16),
            pltpu.VMEM((size, rows, width), BF16),
            pltpu.VMEM((size - 1, rows, width), BF16),
            pltpu.SemaphoreType.DMA((size - 1,)),
            pltpu.SemaphoreType.DMA((size - 1,)),
        ],
        compiler_params=pltpu.CompilerParams(
            collective_id=2, has_side_effects=True, vmem_limit_bytes=32 << 20
        ),
    )(q, kv_all, gate, bias_slots, w)


def shards(
    pair_trunk,
    token_ids,
    w_rel,
    cat_gain,
    w_in,
    trans_gain,
    trans_ab,
    trans_out,
    bias_gain,
    w_bias,
    normed,
    w_proj,
    output_weight,
):
    q_rows = pair_trunk.shape[0]
    k_rows = pair_trunk.shape[1]
    k_start = lax.axis_index("ka") * k_rows
    key_ids = lax.dynamic_slice_in_dim(token_ids, k_start, k_rows, 1)
    key_cols = jnp.broadcast_to(key_ids[:, :, None], (3, k_rows, 128))
    samples = normed.shape[0]
    feat_local = normed.shape[2]
    q, kv, gate = gather_call(normed, w_proj)
    pair_cond, bias_slots, kv_all = pair_call(
        token_ids, key_cols, pair_trunk, w_rel, cat_gain, w_in, trans_gain, trans_ab, trans_out,
        bias_gain, w_bias, kv,
    )
    update = reduce_call(q, kv_all, gate, bias_slots, output_weight)
    return (pair_cond, update.reshape(samples, q_rows, feat_local))


def solution(mesh):
    in_specs = (
        P("pb", "ka", None),
        P(),
        P(),
        P(),
        P(),
        P(),
        P(),
        P(),
        P(),
        P(),
        P(None, "pb", "ka"),
        P(None, None, "ka"),
        P("ka", None),
    )
    out_specs = (P("pb", "ka", None), P(None, "pb", "ka"))
    return jax.shard_map(shards, mesh=mesh, in_specs=in_specs, out_specs=out_specs, check_vma=False)
```
